32 devices in a mesh: wide: 8 (over y, x, core), seq: 4 (over z).
Axes of the slice: x: 2, y: 2, z: 4, core: 2. Of those that a mesh axis runs over, the one named last changes fastest.
Arguments:
- frames: bfloat16 [16384, 768], P(('wide', 'seq')), may hold values from -6 to 6
- cotangent: bfloat16 [16384, 768], P(('wide', 'seq')), may hold values from -6 to 6
- qkv_weight: float32 [2, 768, 2304], P(None, 'wide'), may hold values from -0.21875 to 0.21875
- proj_weight: float32 [2, 768, 768], P(None, 'wide'), may hold values from -0.21875 to 0.21875
- up_weight: float32 [2, 768, 3072], P(None, 'wide'), may hold values from -0.21875 to 0.21875
- down_weight: float32 [2, 3072, 768], P(None, 'wide'), may hold values from -0.109375 to 0.109375
- vectors: float32 [2, 8, 768], P(None, None, 'wide'), may hold values from -1.8 to 1.8, as said below
- up_bias: float32 [2, 3072], P(None, 'wide'), may hold values from -4 to 4
- moment_qkv: float32 [2, 768, 2304], P(None, 'wide'), may hold values from -6 to 6
- moment_proj: float32 [2, 768, 768], P(None, 'wide'), may hold values from -6 to 6
- moment_up: float32 [2, 768, 3072], P(None, 'wide'), may hold values from -6 to 6
- moment_down: float32 [2, 3072, 768], P(None, 'wide'), may hold values from -6 to 6
- moment_vectors: float32 [2, 8, 768], P(None, None, 'wide'), may hold values from -6 to 6
- moment_bias: float32 [2, 3072], P(None, 'wide'), may hold values from -6 to 6
- square_qkv: float32 [2, 768, 2304], P(None, 'wide'), may hold values from 0.1 to 10
- square_proj: float32 [2, 768, 768], P(None, 'wide'), may hold values from 0.1 to 10
- square_up: float32 [2, 768, 3072], P(None, 'wide'), may hold values from 0.1 to 10
- square_down: float32 [2, 3072, 768], P(None, 'wide'), may hold values from 0.1 to 10
- square_vectors: float32 [2, 8, 768], P(None, None, 'wide'), may hold values from 0.1 to 10
- square_bias: float32 [2, 3072], P(None, 'wide'), may hold values from 0.1 to 10
Outputs:
- block_out: float32 [16384, 768], P(('wide', 'seq'))
- frames_grad: float32 [16384, 768], P(('wide', 'seq'))
- qkv_grad: float32 [2, 768, 2304], P(None, 'wide')
- proj_grad: float32 [2, 768, 768], P(None, 'wide')
- up_grad: float32 [2, 768, 3072], P(None, 'wide')
- down_grad: float32 [2, 3072, 768], P(None, 'wide')
- vectors_grad: float32 [2, 8, 768], P(None, None, 'wide')
- bias_grad: float32 [2, 3072], P(None, 'wide')
- new_qkv: float32 [2, 768, 2304], P(None, 'wide')
- new_proj: float32 [2, 768, 768], P(None, 'wide')
- new_up: float32 [2, 768, 3072], P(None, 'wide')
- new_down: float32 [2, 3072, 768], P(None, 'wide')
- new_vectors: float32 [2, 8, 768], P(None, None, 'wide')
- new_bias: float32 [2, 3072], P(None, 'wide')
- new_moment_qkv: float32 [2, 768, 2304], P(None, 'wide')
- new_moment_proj: float32 [2, 768, 768], P(None, 'wide')
- new_moment_up: float32 [2, 768, 3072], P(None, 'wide')
- new_moment_down: float32 [2, 3072, 768], P(None, 'wide')
- new_moment_vectors: float32 [2, 8, 768], P(None, None, 'wide')
- new_moment_bias: float32 [2, 3072], P(None, 'wide')
- new_square_qkv: float32 [2, 768, 2304], P(None, 'wide')
- new_square_proj: float32 [2, 768, 768], P(None, 'wide')
- new_square_up: float32 [2, 768, 3072], P(None, 'wide')
- new_square_down: float32 [2, 3072, 768], P(None, 'wide')
- new_square_vectors: float32 [2, 8, 768], P(None, None, 'wide')
- new_square_bias: float32 [2, 3072], P(None, 'wide')
The draws below stay inside these ranges and needn't reach their ends.
Inputs may be any that keep to these rules, and one draw needn't show every extreme that they name: Rows 0 and 5 of each layer's vectors lie between 0.5 and 1.5.
All inputs are finite; a program needn't handle non-finite values.
Results may differ from the reference program's by a relative error of at most 0.023.
Values may be sent and summed in bfloat16 or wider, within the bound.
No kernel may reach another device: no remote copies, remote signals or barrier semaphores. Data moves between devices by JAX's collectives and lax.ppermute only.
A program may use at most 256 MiB of HBM per device.

```python
import math
import jax
import jax.numpy as jnp
from jax import lax

D = 768
FF = 3072
HEAD_DIM = 64
LAYERS = 2
STEP = 4
SEQ_LEN = 2048
TOKENS = 16384
N_WIDE = 8


def draw_vectors(key, part):
    key_gain, key_shift = jax.random.split(key)
    gains = jax.random.uniform(key_gain, (LAYERS, 8, D), jnp.float32, 0.5, 1.5)
    shifts = 0.3 * jnp.clip(jax.random.normal(key_shift, (LAYERS, 8, D), jnp.float32), -6.0, 6.0)
    row_ids = jnp.arange(8)
    gain_rows = (row_ids == 0) | (row_ids == 5)
    return jnp.where(gain_rows[None, :, None], gains, shifts)


def levels(rng, dims, shards, low, top_value):
    def one(dim, parts):
        draws = jax.random.uniform(jax.random.fold_in(jax.random.fold_in(rng, 6), dim), (parts,), jnp.float32, low / len(shards), top_value / len(shards))
        return jnp.repeat(jnp.exp(draws), dims[dim] // parts).reshape((-1,) + (1,) * (len(dims) - dim - 1))

    level = one(*shards[0])
    for cut in shards[1:]:
        level = level * one(*cut)
    return level


def bell_draw(rng, extent, scale, most, cuts=(), dtype=jnp.bfloat16):
    drawn = jax.random.normal(rng, extent, jnp.float32) * scale
    if len(cuts) > 0:
        drawn = levels(rng, extent, cuts, -0.22, 0.18) * drawn
    return jnp.clip(drawn, min=-most, max=most).astype(dtype)


def setup_inputs(seed: int = 0) -> dict:
    splits = jax.random.split(jax.random.key(seed), 21)
    return {
        "frames": bell_draw(splits[0], (TOKENS, D), 1.0, 6.0, ((0, 32),)),
        "cotangent": bell_draw(splits[1], (TOKENS, D), 1.0, 6.0, ((0, 32),)),
        "qkv_weight": bell_draw(splits[2], (LAYERS, D, 3 * D), D ** -0.5, 0.21875, ((1, 8),), jnp.float32),
        "proj_weight": bell_draw(splits[3], (LAYERS, D, D), D ** -0.5, 0.21875, ((1, 8),), jnp.float32),
        "up_weight": bell_draw(splits[4], (LAYERS, D, FF), D ** -0.5, 0.21875, ((1, 8),), jnp.float32),
        "down_weight": bell_draw(splits[5], (LAYERS, FF, D), FF ** -0.5, 0.109375, ((1, 8),), jnp.float32),
        "vectors": draw_vectors(jax.random.fold_in(splits[20], 71), 0),
        "up_bias": bell_draw(splits[7], (LAYERS, FF), 0.3, 4.0, ((1, 8),), jnp.float32),
        "moment_qkv": bell_draw(splits[8], (LAYERS, D, 3 * D), 1.0, 6.0, ((1, 8),), jnp.float32),
        "moment_proj": bell_draw(splits[9], (LAYERS, D, D), 1.0, 6.0, ((1, 8),), jnp.float32),
        "moment_up": bell_draw(splits[10], (LAYERS, D, FF), 1.0, 6.0, ((1, 8),), jnp.float32),
        "moment_down": bell_draw(splits[11], (LAYERS, FF, D), 1.0, 6.0, ((1, 8),), jnp.float32),
        "moment_vectors": bell_draw(splits[12], (LAYERS, 8, D), 1.0, 6.0, ((2, 8),), jnp.float32),
        "moment_bias": bell_draw(splits[13], (LAYERS, FF), 1.0, 6.0, ((1, 8),), jnp.float32),
        "square_qkv": jnp.clip(jnp.exp(math.log(10.0) - 4.6051702 * jax.random.uniform(splits[14], (LAYERS, D, 3 * D), jnp.float32) ** levels(splits[14], (LAYERS, D, 3 * D), ((1, 8),), -0.2, 0.2)), 0.1, 10.0),
        "square_proj": jnp.clip(jnp.exp(math.log(10.0) - 4.6051702 * jax.random.uniform(splits[15], (LAYERS, D, D), jnp.float32) ** levels(splits[15], (LAYERS, D, D), ((1, 8),), -0.2, 0.2)), 0.1, 10.0),
        "square_up": jnp.clip(jnp.exp(math.log(10.0) - 4.6051702 * jax.random.uniform(splits[16], (LAYERS, D, FF), jnp.float32) ** levels(splits[16], (LAYERS, D, FF), ((1, 8),), -0.2, 0.2)), 0.1, 10.0),
        "square_down": jnp.clip(jnp.exp(math.log(10.0) - 4.6051702 * jax.random.uniform(splits[17], (LAYERS, FF, D), jnp.float32) ** levels(splits[17], (LAYERS, FF, D), ((1, 8),), -0.2, 0.2)), 0.1, 10.0),
        "square_vectors": jnp.clip(jnp.exp(math.log(10.0) - 4.6051702 * jax.random.uniform(splits[18], (LAYERS, 8, D), jnp.float32) ** levels(splits[18], (LAYERS, 8, D), ((2, 8),), -0.2, 0.2)), 0.1, 10.0),
        "square_bias": jnp.clip(jnp.exp(math.log(10.0) - 4.6051702 * jax.random.uniform(splits[19], (LAYERS, FF), jnp.float32) ** levels(splits[19], (LAYERS, FF), ((1, 8),), -0.2, 0.2)), 0.1, 10.0),
    }


norm_eps = 1e-05
score_scale = 0.125
beta_one = 0.9
beta_two = 0.999
adam_eps = 1e-08
learn_rate = 0.02
decay_rate = 0.1

def inner_rows(left, right):
    return jnp.dot(left.T, right, preferred_element_type=jnp.float32)

def outer_cols(left, right):
    return jnp.dot(left, right.T, preferred_element_type=jnp.float32)

def layer_norm(values, gain, shift):
    centred = values - lax.optimization_barrier(jnp.mean(values, axis=1, keepdims=True))
    inv_sigma = lax.rsqrt(lax.optimization_barrier(jnp.mean(centred * centred, axis=1, keepdims=True)) + norm_eps)
    normal_part = centred * inv_sigma
    return (normal_part * gain + shift, normal_part, inv_sigma)

def norm_back(grad_in, normal_part, inv_sigma, gain):
    scaled = grad_in * gain
    grad_values = inv_sigma * (scaled - lax.optimization_barrier(jnp.mean(scaled, axis=1, keepdims=True)) - normal_part * lax.optimization_barrier(jnp.mean(scaled * normal_part, axis=1, keepdims=True)))
    return (grad_values, lax.optimization_barrier(jnp.sum(grad_in * normal_part, axis=0)), lax.optimization_barrier(jnp.sum(grad_in, axis=0)))

def gelu_value(pre_act):
    return 0.5 * pre_act * (1.0 + lax.erf(pre_act * 0.7071067811865476))

def gelu_slope(pre_act):
    return 0.5 * (1.0 + lax.erf(pre_act * 0.7071067811865476)) + pre_act * jnp.exp(-0.5 * pre_act * pre_act) * 0.3989422804014327

def block_rows(length):
    return 512 if length % 512 == 0 else length

def attend_forward(queries, key_rows, value_rows):
    length = queries.shape[0]
    head_count = queries.shape[1] // HEAD_DIM
    block_len = block_rows(length)
    key_heads = key_rows.astype(jnp.float32).reshape(length, head_count, HEAD_DIM)
    value_heads = value_rows.astype(jnp.float32).reshape(length, head_count, HEAD_DIM)
    query_blocks = queries.astype(jnp.float32).reshape(length // block_len, block_len, head_count, HEAD_DIM)

    def one_block(query_blk):
        scores = jnp.einsum('qhd,khd->hqk', query_blk, key_heads) * score_scale
        totals = jnp.log(lax.optimization_barrier(jnp.sum(jnp.exp(scores), axis=2)))
        weights_bf = jnp.exp(scores - totals[:, :, None]).astype(jnp.bfloat16)
        mixed_blk = jnp.einsum('hqk,khd->qhd', weights_bf.astype(jnp.float32), value_heads)
        return (mixed_blk.astype(jnp.bfloat16), totals)
    mixed_all, totals = lax.map(one_block, query_blocks)
    return (mixed_all.reshape(length, head_count * HEAD_DIM), totals)

def attend_backward(queries, key_rows, value_rows, mixed_rows, totals, grad_rows):
    length = queries.shape[0]
    head_count = queries.shape[1] // HEAD_DIM
    block_len = block_rows(length)
    count_blocks = length // block_len
    key_heads = key_rows.astype(jnp.float32).reshape(length, head_count, HEAD_DIM)
    value_heads = value_rows.astype(jnp.float32).reshape(length, head_count, HEAD_DIM)

    def shaped(member):
        return member.astype(jnp.float32).reshape(count_blocks, block_len, head_count, HEAD_DIM)

    def one_block(running, inputs):
        key_grad, value_grad = running
        query_blk, mixed_blk, grad_blk, total_blk = inputs
        scores = jnp.einsum('qhd,khd->hqk', query_blk, key_heads) * score_scale
        prob_vals = jnp.exp(scores - total_blk[:, :, None])
        prob_bf = prob_vals.astype(jnp.bfloat16).astype(jnp.float32)
        value_grad = value_grad + jnp.einsum('hqk,qhd->khd', prob_bf, grad_blk)
        prob_grad = jnp.einsum('qhd,khd->hqk', grad_blk, value_heads)
        row_dots = jnp.einsum('qhd,qhd->hq', grad_blk, mixed_blk)
        score_grad = (prob_vals * (prob_grad - row_dots[:, :, None]) * score_scale).astype(jnp.bfloat16)
        score_f = score_grad.astype(jnp.float32)
        query_grad = jnp.einsum('hqk,khd->qhd', score_f, key_heads).astype(jnp.bfloat16)
        key_grad = key_grad + jnp.einsum('hqk,qhd->khd', score_f, query_blk)
        return ((key_grad, value_grad), query_grad)
    zero_heads = jnp.zeros((length, head_count, HEAD_DIM), jnp.float32)
    (key_grad, value_grad), query_grad = lax.scan(one_block, (zero_heads, zero_heads), (shaped(queries), shaped(mixed_rows), shaped(grad_rows), totals))
    flat_width = head_count * HEAD_DIM
    return (query_grad.reshape(length, flat_width), key_grad.astype(jnp.bfloat16).reshape(length, flat_width), value_grad.astype(jnp.bfloat16).reshape(length, flat_width))

def layer_forward(resid_in, params):
    w_qkv, w_out, w_up, w_down, vec_rows, bias_up = params
    model_dim = resid_in.shape[1]
    normed_one, hat_one, sigma_one = layer_norm(resid_in, vec_rows[0], vec_rows[1])
    normed_one = normed_one.astype(jnp.bfloat16)
    projected = jnp.dot(normed_one, w_qkv, preferred_element_type=jnp.float32)
    query_tok = (projected[:, :model_dim] + vec_rows[2]).astype(jnp.bfloat16)
    key_tok = projected[:, model_dim:2 * model_dim].astype(jnp.bfloat16)
    value_tok = (projected[:, 2 * model_dim:] + vec_rows[3]).astype(jnp.bfloat16)
    mixed_tok, totals = attend_forward(query_tok, key_tok, value_tok)
    resid_mid = resid_in + jnp.dot(mixed_tok, w_out, preferred_element_type=jnp.float32) + vec_rows[4]
    normed_two, hat_two, sigma_two = layer_norm(resid_mid, vec_rows[5], vec_rows[6])
    normed_two = normed_two.astype(jnp.bfloat16)
    pre_act = jnp.dot(normed_two, w_up, preferred_element_type=jnp.float32) + bias_up
    activated = gelu_value(pre_act).astype(jnp.bfloat16)
    resid_out = resid_mid + jnp.dot(activated, w_down, preferred_element_type=jnp.float32) + vec_rows[7]
    saved = (hat_one, sigma_one, normed_one, query_tok, key_tok, value_tok, mixed_tok, totals, hat_two, sigma_two, normed_two, pre_act, activated)
    return (resid_out, saved)

def layer_backward(grad_out, params, saved):
    w_qkv, w_out, w_up, w_down, vec_rows, bias_up = params
    hat_one, sigma_one, normed_one, query_tok, key_tok, value_tok, mixed_tok, totals, hat_two, sigma_two, normed_two, pre_act, activated = saved
    grad_bf = grad_out.astype(jnp.bfloat16)
    grad_down = inner_rows(activated, grad_bf)
    grad_act = outer_cols(grad_bf, w_down)
    grad_pre = grad_act * gelu_slope(pre_act)
    grad_bias_up = lax.optimization_barrier(jnp.sum(grad_pre, axis=0))
    grad_pre_bf = grad_pre.astype(jnp.bfloat16)
    grad_up = inner_rows(normed_two, grad_pre_bf)
    grad_normed_two = outer_cols(grad_pre_bf, w_up)
    grad_mid_norm, gain_two_grad, shift_two_grad = norm_back(grad_normed_two, hat_two, sigma_two, vec_rows[5])
    grad_mid = grad_out + grad_mid_norm
    grad_mid_bf = grad_mid.astype(jnp.bfloat16)
    grad_wout = inner_rows(mixed_tok, grad_mid_bf)
    grad_mixed = outer_cols(grad_mid_bf, w_out).astype(jnp.bfloat16)
    grad_query, grad_key, grad_value = attend_backward(query_tok, key_tok, value_tok, mixed_tok, totals, grad_mixed)
    grad_proj = jnp.concatenate((grad_query, grad_key, grad_value), axis=1)
    grad_wqkv = inner_rows(normed_one, grad_proj)
    grad_normed_one = outer_cols(grad_proj, w_qkv)
    grad_in_norm, gain_one_grad, shift_one_grad = norm_back(grad_normed_one, hat_one, sigma_one, vec_rows[0])
    grad_in = grad_mid + grad_in_norm
    grad_vectors = jnp.stack((gain_one_grad, shift_one_grad, lax.optimization_barrier(jnp.sum(grad_query.astype(jnp.float32), axis=0)), lax.optimization_barrier(jnp.sum(grad_value.astype(jnp.float32), axis=0)), lax.optimization_barrier(jnp.sum(grad_mid, axis=0)), gain_two_grad, shift_two_grad, lax.optimization_barrier(jnp.sum(grad_out, axis=0))))
    return (grad_in, (grad_wqkv, grad_wout, grad_up, grad_down, grad_vectors, grad_bias_up))

def adam_step(weight, moment, square, grad):
    moment_new = beta_one * moment + (1.0 - beta_one) * grad
    square_new = beta_two * square + (1.0 - beta_two) * grad * grad
    moment_hat = moment_new / (1.0 - beta_one ** STEP)
    square_hat = square_new / (1.0 - beta_two ** STEP)
    weight_new = weight - learn_rate * (moment_hat / (jnp.sqrt(square_hat) + adam_eps) + decay_rate * weight)
    return (weight_new, moment_new, square_new)

def round_trip(member):
    return lax.optimization_barrier(member.astype(jnp.bfloat16)).astype(jnp.float32)

def reference(frames, cotangent, qkv_weight, proj_weight, up_weight, down_weight, vectors, up_bias, moment_qkv, moment_proj, moment_up, moment_down, moment_vectors, moment_bias, square_qkv, square_proj, square_up, square_down, square_vectors, square_bias):
    layer_params = []
    for layer_pos in range(LAYERS):
        layer_params.append((qkv_weight[layer_pos].astype(jnp.bfloat16), proj_weight[layer_pos].astype(jnp.bfloat16), up_weight[layer_pos].astype(jnp.bfloat16), down_weight[layer_pos].astype(jnp.bfloat16), round_trip(vectors[layer_pos]), round_trip(up_bias[layer_pos])))
    frame_clips = frames.reshape(N_WIDE, SEQ_LEN, D)
    cot_clips = cotangent.reshape(N_WIDE, SEQ_LEN, D)

    def zero_layer():
        return (jnp.zeros((D, 3 * D), jnp.float32), jnp.zeros((D, D), jnp.float32), jnp.zeros((D, FF), jnp.float32), jnp.zeros((FF, D), jnp.float32), jnp.zeros((8, D), jnp.float32), jnp.zeros((FF,), jnp.float32))

    def one_clip(running, clip_in):
        clip_frames, clip_cot = clip_in
        resid = clip_frames.astype(jnp.float32)
        saved_list = []
        for layer_pos in range(LAYERS):
            resid, saved = layer_forward(resid, layer_params[layer_pos])
            saved_list.append(saved)
        grad_resid = clip_cot.astype(jnp.float32)
        new_running = list(running)
        for layer_pos in reversed(range(LAYERS)):
            grad_resid, grads = layer_backward(grad_resid, layer_params[layer_pos], saved_list[layer_pos])
            new_running[layer_pos] = tuple((total + term for total, term in zip(running[layer_pos], grads)))
        return (tuple(new_running), (resid, grad_resid))
    init_sums = tuple((zero_layer() for layer_pos in range(LAYERS)))
    grad_sums, (clip_out, clip_grad) = lax.scan(one_clip, init_sums, (frame_clips, cot_clips))
    block_out = clip_out.reshape(TOKENS, D)
    frames_grad = clip_grad.reshape(TOKENS, D)
    stacked = [jnp.stack([grad_sums[layer_pos][member_pos] for layer_pos in range(LAYERS)]) for member_pos in range(6)]
    weights_in = (qkv_weight, proj_weight, up_weight, down_weight, vectors, up_bias)
    moments_in = (moment_qkv, moment_proj, moment_up, moment_down, moment_vectors, moment_bias)
    squares_in = (square_qkv, square_proj, square_up, square_down, square_vectors, square_bias)
    new_weights, new_moments, new_squares = ([], [], [])
    for member_pos in range(6):
        weight_new, moment_new, square_new = adam_step(weights_in[member_pos], moments_in[member_pos], squares_in[member_pos], stacked[member_pos])
        new_weights.append(weight_new)
        new_moments.append(moment_new)
        new_squares.append(square_new)
    return (block_out, frames_grad, stacked[0], stacked[1], stacked[2], stacked[3], stacked[4], stacked[5], new_weights[0], new_weights[1], new_weights[2], new_weights[3], new_weights[4], new_weights[5], new_moments[0], new_moments[1], new_moments[2], new_moments[3], new_moments[4], new_moments[5], new_squares[0], new_squares[1], new_squares[2], new_squares[3], new_squares[4], new_squares[5])
```

```python
import functools
import math

import jax
import jax.numpy as jnp
from jax import lax
from jax.experimental import pallas as pl
from jax.experimental.pallas import tpu as pltpu
from jax.sharding import Mesh
from jax.sharding import PartitionSpec as P

HEAD_DIM = 64
LAYERS = 2
STEP = 4

norm_eps = 1e-05
score_scale = 0.125
beta_one = 0.9
beta_two = 0.999
adam_eps = 1e-08
learn_rate = 0.02
decay_rate = 0.1
LOG2E = math.log2(math.e)

bf16 = jnp.bfloat16
f32 = jnp.float32


def dotg(left, right, cl, cr):
    return lax.dot_general(left, right, (((cl,), (cr,)), ((), ())), preferred_element_type=f32)


def attn_fwd_kernel(q_ref, k_ref, v_ref, o_ref, l_ref, vt_ref, *, heads):
    rows = q_ref.shape[0]

    @pl.when(pl.program_id(0) == 0)
    def _():
        for h in range(heads):
            sl = slice(h * HEAD_DIM, (h + 1) * HEAD_DIM)
            vt_ref[h, :HEAD_DIM, :] = v_ref[:, sl].T
            vt_ref[h, HEAD_DIM:, :] = jnp.ones((vt_ref.shape[1] - HEAD_DIM, vt_ref.shape[2]), bf16)

    l_ref[...] = jnp.zeros_like(l_ref)
    for h in range(heads):
        sl = slice(h * HEAD_DIM, (h + 1) * HEAD_DIM)
        scores = dotg(k_ref[:, sl], q_ref[:, sl], 1, 1)
        expo = jnp.exp2(scores).astype(bf16)
        acc = dotg(vt_ref[h], expo, 1, 0)
        total = acc[HEAD_DIM : HEAD_DIM + 1, :]
        o_ref[:, sl] = (acc[:HEAD_DIM, :] / total).T.astype(bf16)
        l_ref[h : h + 1, :] = jnp.log2(total)


def attn_fwd(q, k, v):
    length, width = q.shape
    heads = width // HEAD_DIM
    bq = length // 4
    return pl.pallas_call(
        functools.partial(attn_fwd_kernel, heads=heads),
        grid=(length // bq,),
        in_specs=[
            pl.BlockSpec((bq, width), lambda i: (i, 0)),
            pl.BlockSpec((length, width), lambda i: (0, 0)),
            pl.BlockSpec((length, width), lambda i: (0, 0)),
        ],
        out_specs=[
            pl.BlockSpec((bq, width), lambda i: (i, 0)),
            pl.BlockSpec((8, bq), lambda i: (0, i)),
        ],
        out_shape=[
            jax.ShapeDtypeStruct((length, width), bf16),
            jax.ShapeDtypeStruct((8, length), f32),
        ],
        scratch_shapes=[pltpu.VMEM((heads, HEAD_DIM + 16, length), bf16)],
        compiler_params=pltpu.CompilerParams(vmem_limit_bytes=60 << 20),
        cost_estimate=pl.CostEstimate(
            flops=16 * length * length * width,
            transcendentals=length * length * heads,
            bytes_accessed=8 * length * width,
        ),
        name="attn_fwd",
    )(q, k, v)


def attn_bwd_kernel(
    q_ref, do_ref, o_ref, l_ref, k_ref, v_ref, dq_ref, dk_ref, dv_ref, dkt_ref, dvt_ref, *, heads
):
    step = pl.program_id(0)

    @pl.when(step == 0)
    def _():
        dkt_ref[...] = jnp.zeros_like(dkt_ref)
        dvt_ref[...] = jnp.zeros_like(dvt_ref)

    lse_cols = l_ref[...].T
    for h in range(heads):
        sl = slice(h * HEAD_DIM, (h + 1) * HEAD_DIM)
        q = q_ref[:, sl]
        do = do_ref[:, sl]
        delta = jnp.sum(do.astype(f32) * o_ref[:, sl].astype(f32), axis=1, keepdims=True)
        k = k_ref[:, sl]
        probs = jnp.exp2(dotg(q, k, 1, 1) - lse_cols[:, h : h + 1])
        dprobs = dotg(do, v_ref[:, sl], 1, 1)
        ds = (probs * (dprobs - delta)).astype(bf16)
        dvt_ref[sl, :] += dotg(do.T, probs.astype(bf16), 1, 0)
        dkt_ref[sl, :] += dotg(q.T, ds, 1, 0)
        dq_ref[:, sl] = (dotg(k.T, ds, 1, 1) * score_scale).T.astype(bf16)

    @pl.when(step == pl.num_programs(0) - 1)
    def _():
        dk_ref[...] = (dkt_ref[...] * (1.0 / LOG2E)).T.astype(bf16)
        dv_ref[...] = dvt_ref[...].T.astype(bf16)


def attn_bwd(q, k, v, o, lse, do):
    length, width = q.shape
    heads = width // HEAD_DIM
    bq = length // 4
    blk = pl.BlockSpec((bq, width), lambda i: (i, 0))
    full = pl.BlockSpec((length, width), lambda i: (0, 0))
    return pl.pallas_call(
        functools.partial(attn_bwd_kernel, heads=heads),
        grid=(length // bq,),
        in_specs=[blk, blk, blk, pl.BlockSpec((8, bq), lambda i: (0, i)), full, full],
        out_specs=[blk, full, full],
        out_shape=[jax.ShapeDtypeStruct((length, width), bf16)] * 3,
        scratch_shapes=[pltpu.VMEM((width, length), f32)] * 2,
        compiler_params=pltpu.CompilerParams(vmem_limit_bytes=60 << 20),
        cost_estimate=pl.CostEstimate(
            flops=40 * length * length * width,
            transcendentals=length * length * heads,
            bytes_accessed=16 * length * width,
        ),
        name="attn_bwd",
    )(q, do, o, lse, k, v)


def layer_norm(values, gain, shift):
    centred = values - jnp.mean(values, axis=1, keepdims=True)
    inv_sigma = lax.rsqrt(jnp.mean(centred * centred, axis=1, keepdims=True) + norm_eps)
    normal_part = centred * inv_sigma
    return (normal_part * gain + shift, normal_part, inv_sigma)


def norm_back(grad_in, normal_part, inv_sigma, gain):
    scaled = grad_in * gain
    grad_values = inv_sigma * (
        scaled
        - jnp.mean(scaled, axis=1, keepdims=True)
        - normal_part * jnp.mean(scaled * normal_part, axis=1, keepdims=True)
    )
    return (grad_values, jnp.sum(grad_in * normal_part, axis=0), jnp.sum(grad_in, axis=0))


def gelu_value(pre_act):
    return 0.5 * pre_act * (1.0 + lax.erf(pre_act * 0.7071067811865476))


def gelu_slope(pre_act):
    return (
        0.5 * (1.0 + lax.erf(pre_act * 0.7071067811865476))
        + pre_act * jnp.exp(-0.5 * pre_act * pre_act) * 0.3989422804014327
    )


def adam_step(weight, moment, square, grad):
    moment_new = beta_one * moment + (1.0 - beta_one) * grad
    square_new = beta_two * square + (1.0 - beta_two) * grad * grad
    moment_hat = moment_new / (1.0 - beta_one**STEP)
    square_hat = square_new / (1.0 - beta_two**STEP)
    weight_new = weight - learn_rate * (
        moment_hat / (jnp.sqrt(square_hat) + adam_eps) + decay_rate * weight
    )
    return (weight_new, moment_new, square_new)


def solution(mesh):
    n_wide, n_seq = mesh.shape["wide"], mesh.shape["seq"]
    bits = n_wide.bit_length() - 1
    wide_axes = tuple("w%d" % i for i in range(bits))
    names = wide_axes + ("sh", "sl")
    dims = (2,) * bits + (2, n_seq // 2)
    inner = Mesh(mesh.devices.reshape(dims), names)
    wl = wide_axes[-1]
    high_axes = wide_axes[:-1]
    n_high = n_wide // 2
    total = n_wide * n_seq

    def coords(flat):
        out = []
        for size in reversed(dims):
            out.append(flat % size)
            flat //= size
        return dict(zip(reversed(names), out))

    def flat_of(at):
        flat = 0
        for name, size in zip(names, dims):
            flat = flat * size + at[name]
        return flat

    def flip_perm(*which):
        pairs = []
        for i in range(total):
            at = coords(i)
            for name in which:
                at[name] ^= 1
            pairs.append((i, flat_of(at)))
        return pairs

    swap_pairs = []
    for i in range(total):
        at = coords(i)
        at[wl], at["sh"] = at["sh"], at[wl]
        swap_pairs.append((i, flat_of(at)))

    def flip(value, *which):
        return lax.ppermute(value, names, flip_perm(*which))

    def swap_tokens(value):
        return lax.ppermute(value, names, swap_pairs)

    def local(
        frames,
        cotangent,
        qkv_weight,
        proj_weight,
        up_weight,
        down_weight,
        vectors,
        up_bias,
        *states,
    ):
        moments_in, squares_in = states[:6], states[6:]
        core = lax.axis_index(wl)
        zlow = lax.axis_index("sl")
        high = lax.axis_index(high_axes)
        hb = core * 2 + zlow
        n_tok, dim = frames.shape
        own_rows = qkv_weight.shape[1]
        hidden = up_weight.shape[2]
        n_up = hidden // dim
        down_rows = down_weight.shape[1]
        blk = dim // n_seq
        wide3 = 3 * blk
        vec_rows = vectors.shape[1]
        vec_len = vec_rows * own_rows + down_rows
        vec_pad = -(-vec_len // (16 * wide3)) * 16

        qkv_bf = qkv_weight.astype(bf16).reshape(LAYERS, own_rows, 3, n_seq, blk)

        def head_cols(which):
            return lax.dynamic_index_in_dim(qkv_bf, which, 3, keepdims=False).reshape(
                LAYERS * own_rows, wide3
            )

        small = [
            jnp.concatenate([vectors[l].reshape(-1), up_bias[l], jnp.zeros((vec_pad * wide3 - vec_len,), f32)])
            .astype(bf16)
            .reshape(vec_pad, wide3)
            for l in range(LAYERS)
        ]
        small = jnp.concatenate(small)
        keep = jnp.concatenate([head_cols(hb), small])
        give = jnp.concatenate([head_cols(hb ^ 2), small])
        got = flip(give, wl)
        first = jnp.where(core == 0, keep, got)
        second = jnp.where(core == 0, got, keep)
        pair = jnp.stack([first, second])
        gathered = lax.all_gather(pair, high_axes, axis=0, tiled=True)
        qkv_own = [
            gathered[:, l * own_rows : (l + 1) * own_rows].reshape(dim, wide3) for l in range(LAYERS)
        ]
        vec_all, bias_all = [], []
        for l in range(LAYERS):
            at = LAYERS * own_rows + l * vec_pad
            flat = gathered[:, at : at + vec_pad].reshape(n_wide, vec_pad * wide3).astype(f32)
            vec_all.append(
                flat[:, : vec_rows * own_rows]
                .reshape(n_wide, vec_rows, own_rows)
                .transpose(1, 0, 2)
                .reshape(vec_rows, dim)
            )
            bias_all.append(flat[:, vec_rows * own_rows : vec_len].reshape(hidden))

        big = []
        for l in range(LAYERS):
            packed = jnp.concatenate(
                [proj_weight[l]]
                + [up_weight[l][:, j * dim : (j + 1) * dim] for j in range(n_up)]
                + [down_weight[l]]
            ).astype(bf16)
            got_big = lax.all_gather(packed[None], wide_axes, axis=0, tiled=True)
            w_out = got_big[:, :own_rows].reshape(dim, dim)
            w_up = [
                got_big[:, (1 + j) * own_rows : (2 + j) * own_rows].reshape(dim, dim)
                for j in range(n_up)
            ]
            w_up = jnp.concatenate(w_up, axis=1)
            w_down = got_big[:, (1 + n_up) * own_rows :].reshape(hidden, dim)
            w_out = w_out.reshape(n_seq, blk, dim)
            w_out = jnp.concatenate(
                [lax.dynamic_index_in_dim(w_out, hb ^ j, 0, keepdims=False) for j in range(n_seq)]
            )
            big.append((w_out, w_up, w_down))

        def rel_gather(value):
            by_z = flip(value, "sl")
            by_core = flip(value, wl)
            by_both = flip(by_z, wl)
            return jnp.concatenate([value, by_z, by_core, by_both])

        def rel_exchange(blocks):
            return [
                blocks[0],
                flip(blocks[1], "sl"),
                flip(blocks[2], wl),
                flip(blocks[3], "sl", wl),
            ]

        resid = swap_tokens(frames).astype(f32)
        cot = swap_tokens(cotangent)
        saved = []
        for l in range(LAYERS):
            w_out, w_up, w_down = big[l]
            vec, bias_up = vec_all[l], bias_all[l]
            n1, hat1, sig1 = layer_norm(resid, vec[0], vec[1])
            n1_all = rel_gather(n1.astype(bf16))
            proj = jnp.dot(n1_all, qkv_own[l], preferred_element_type=f32)
            q_bias = lax.dynamic_slice(vec[2], (hb * blk,), (blk,))
            v_bias = lax.dynamic_slice(vec[3], (hb * blk,), (blk,))
            q = ((proj[:, :blk] + q_bias) * (score_scale * LOG2E)).astype(bf16)
            k = proj[:, blk : 2 * blk].astype(bf16)
            v = (proj[:, 2 * blk :] + v_bias).astype(bf16)
            o, lse = attn_fwd(q, k, v)
            mixed = jnp.concatenate(
                rel_exchange([o[j * n_tok : (j + 1) * n_tok] for j in range(n_seq)]), axis=1
            )
            mid = resid + jnp.dot(mixed, w_out, preferred_element_type=f32) + vec[4]
            n2, hat2, sig2 = layer_norm(mid, vec[5], vec[6])
            n2 = n2.astype(bf16)
            pre = jnp.dot(n2, w_up, preferred_element_type=f32) + bias_up
            act = gelu_value(pre).astype(bf16)
            resid = mid + jnp.dot(act, w_down, preferred_element_type=f32) + vec[7]
            saved.append((hat1, sig1, n1_all, q, k, v, o, lse, mixed, hat2, sig2, n2, pre, act))
        block_out = swap_tokens(resid.astype(bf16)).astype(f32)

        grad = cot.astype(f32)
        owned = [None] * LAYERS
        for l in reversed(range(LAYERS)):
            w_out, w_up, w_down = big[l]
            vec = vec_all[l]
            hat1, sig1, n1_all, q, k, v, o, lse, mixed, hat2, sig2, n2, pre, act = saved[l]
            grad_bf = grad.astype(bf16)
            d_down = dotg(act, grad_bf, 0, 0)
            d_pre = dotg(grad_bf, w_down, 1, 1) * gelu_slope(pre)
            d_bias = jnp.sum(d_pre, axis=0)
            d_pre_bf = d_pre.astype(bf16)
            d_up = dotg(n2, d_pre_bf, 0, 0)
            d_n2 = dotg(d_pre_bf, w_up, 1, 1)
            back2, gain2, shift2 = norm_back(d_n2, hat2, sig2, vec[5])
            g1 = grad + back2
            g1_bf = g1.astype(bf16)
            d_mixed = dotg(g1_bf, w_out, 1, 1).astype(bf16)
            do = jnp.concatenate(
                rel_exchange([d_mixed[:, j * blk : (j + 1) * blk] for j in range(n_seq)])
            )
            d_out = dotg(mixed, g1_bf, 0, 0).astype(bf16).reshape(n_seq, blk, dim)
            d_out = jnp.concatenate(
                [lax.dynamic_index_in_dim(d_out, hb ^ j, 0, keepdims=False) for j in range(n_seq)]
            )
            packed = jnp.concatenate(
                [d_out.reshape(n_wide, own_rows, dim)]
                + [
                    d_up[:, j * dim : (j + 1) * dim].astype(bf16).reshape(n_wide, own_rows, dim)
                    for j in range(n_up)
                ]
                + [d_down.astype(bf16).reshape(n_wide, down_rows, dim)],
                axis=1,
            )
            mine = lax.psum_scatter(packed, wide_axes, scatter_dimension=0, tiled=False)
            half = mine.shape[0] // 2
            low, top = mine[:half], mine[half:]
            stay = jnp.where(zlow == 0, low, top)
            send = jnp.where(zlow == 0, top, low)
            stay = (stay.astype(f32) + flip(send, "sl").astype(f32)).astype(bf16)
            stay = (stay.astype(f32) + flip(stay, "sh").astype(f32)).astype(bf16)
            other = flip(stay, "sl")
            mine = jnp.concatenate(
                [jnp.where(zlow == 0, stay, other), jnp.where(zlow == 0, other, stay)]
            )

            dq, dk, dv = attn_bwd(q, k, v, o, lse, do)
            dp3 = jnp.concatenate([dq, dk, dv], axis=1)
            part = dotg(dp3, qkv_own[l], 1, 1)
            part_bf = part.astype(bf16)
            got_own = flip(part_bf[2 * n_tok : 3 * n_tok], wl)
            got_far = flip(part_bf[3 * n_tok :], wl)
            far = (part[n_tok : 2 * n_tok] + got_far.astype(f32)).astype(bf16)
            d_n1 = part[:n_tok] + got_own.astype(f32) + flip(far, "sl").astype(f32)
            back1, gain1, shift1 = norm_back(d_n1, hat1, sig1, vec[0])
            d_own = dotg(n1_all, dp3, 0, 0).astype(bf16).reshape(n_wide, own_rows, wide3)

            def place(value):
                return lax.dynamic_update_slice(jnp.zeros((dim,), f32), value, (hb * blk,))

            d_vec = jnp.stack(
                (
                    gain1,
                    shift1,
                    place(jnp.sum(dq.astype(f32), axis=0)),
                    place(jnp.sum(dv.astype(f32), axis=0)),
                    jnp.sum(g1, axis=0),
                    gain2,
                    shift2,
                    jnp.sum(grad, axis=0),
                )
            )
            grad = g1 + back1
            d_small = jnp.concatenate(
                [
                    d_vec.reshape(vec_rows, n_wide, own_rows)
                    .transpose(1, 0, 2)
                    .reshape(n_wide, vec_rows * own_rows),
                    d_bias.reshape(n_wide, down_rows),
                    jnp.zeros((n_wide, vec_pad * wide3 - vec_len), f32),
                ],
                axis=1,
            )
            tail = jnp.concatenate(
                [d_own, d_small.astype(bf16).reshape(n_wide, vec_pad, wide3)], axis=1
            )
            tail_rows = tail.shape[1]
            for name in high_axes:
                half_owners = tail.shape[0] // 2
                bit = lax.axis_index(name)
                low, top = tail[:half_owners], tail[half_owners:]
                stay = jnp.where(bit == 0, low, top)
                send = jnp.where(bit == 0, top, low)
                tail = (stay.astype(f32) + flip(send, name).astype(f32)).astype(bf16)
            tail = (tail.astype(f32) + flip(tail, "sh").astype(f32)).astype(bf16)
            stay = jnp.where(core == 0, tail[0], tail[1])
            send = jnp.where(core == 0, tail[1], tail[0])
            duo = jnp.stack([stay, flip(send, wl)])
            quad = jnp.concatenate([duo, flip(duo, "sl")])
            by_mask = [quad[0], quad[2], quad[1], quad[3]]
            by_block = []
            for a in range(n_seq):
                mask = hb ^ a
                by_block.append(lax.select_n(mask, *by_mask))
            own_qkv = jnp.stack([b[:own_rows] for b in by_block])
            own_qkv = (
                own_qkv.reshape(n_seq, own_rows, 3, blk)
                .transpose(1, 2, 0, 3)
                .reshape(own_rows, 3 * dim)
                .astype(f32)
            )
            own_small = sum(b[own_rows:].astype(f32) for b in by_block).reshape(-1)
            own_vec = own_small[: vec_rows * own_rows].reshape(vec_rows, own_rows)
            own_bias = own_small[vec_rows * own_rows : vec_len]
            own_out = mine[:own_rows].astype(f32)
            own_up = jnp.concatenate(
                [mine[(1 + j) * own_rows : (2 + j) * own_rows] for j in range(n_up)], axis=1
            ).astype(f32)
            own_down = mine[(1 + n_up) * own_rows :].astype(f32)
            owned[l] = (own_qkv, own_out, own_up, own_down, own_vec, own_bias)
        frames_grad = swap_tokens(grad.astype(bf16)).astype(f32)

        stacked = [jnp.stack([owned[l][m] for l in range(LAYERS)]) for m in range(6)]
        weights_in = (qkv_weight, proj_weight, up_weight, down_weight, vectors, up_bias)
        new_weights, new_moments, new_squares = [], [], []
        for m in range(6):
            weight_new, moment_new, square_new = adam_step(
                weights_in[m], moments_in[m], squares_in[m], stacked[m]
            )
            new_weights.append(weight_new)
            new_moments.append(moment_new)
            new_squares.append(square_new)
        return (block_out, frames_grad, *stacked, *new_weights, *new_moments, *new_squares)

    rows = P(wide_axes + ("sh", "sl"), None)
    mat = P(None, wide_axes, None)
    param_specs = (mat, mat, mat, mat, P(None, None, wide_axes), P(None, wide_axes))
    return jax.shard_map(
        local,
        mesh=inner,
        in_specs=(rows, rows) + param_specs * 3,
        out_specs=(rows, rows) + param_specs * 4,
        check_vma=False,
    )
```
